128 devices in a mesh: rack: 16 (over z, x_hi, core), cls: 8 (over x_lo, y).
Axes of the slice: x: 4 (x_hi: 2, x_lo: 2; x = x_hi * 2 + x_lo), y: 4, z: 4, core: 2. Of those that a mesh axis runs over, the one named last changes fastest.
Arguments:
- history: bfloat16 [4, 5120, 5120], P(None, 'rack', 'cls'), may hold values from -6 to 6
- rack_lag_coefficients: float32 [4, 5120], P(None, 'rack'), may hold values from -4 to 4
- class_lag_coefficients: float32 [4, 5120], P(None, 'cls'), may hold values from -4 to 4
- rack_reconcile_matrix: float32 [5120, 5120], P('rack', 'cls'), may hold values from -1 to 1
- class_reconcile_matrix: float32 [5120, 5120], P('rack', 'cls'), may hold values from -1 to 1
Outputs:
- reconciled: float32 [5120, 5120], P('rack', 'cls')
The draws below stay inside these ranges and needn't reach their ends.
All inputs are finite; a program needn't handle non-finite values.
Results may differ from the reference program's by a relative error of at most 0.0003.
Values sent between devices are 32-bit elements; how exact they have to be, the bound alone decides.
No kernel may reach another device: no remote copies, remote signals or barrier semaphores. Data moves between devices by JAX's collectives and lax.ppermute only.
A program may use at most 128 MiB of HBM per device.

```python
import math
import jax
import jax.numpy as jnp
from jax import lax

NR = 5120
NC = 5120
LAGS = 4


def projection_like(key, order):
    key_off, key_diag = jax.random.split(key)
    row_ids = lax.broadcasted_iota(jnp.int32, (order, order), 0)
    col_ids = lax.broadcasted_iota(jnp.int32, (order, order), 1)
    offdiag = jax.random.normal(key_off, (order, order), jnp.float32) * (0.6 / math.sqrt(order))
    offdiag = jnp.clip(offdiag, -0.9, 0.9)
    diag_vals = jax.random.uniform(key_diag, (order, order), jnp.float32, 0.5, 1.0)
    return jnp.where(row_ids == col_ids, diag_vals, offdiag)


def draw_rack_reconcile_matrix(key, part):
    return projection_like(jax.random.fold_in(key, 11), NR)


def draw_class_reconcile_matrix(key, part):
    return projection_like(jax.random.fold_in(key, 23), NC)


def steps_of(rng, dims, cuts, low, top_value):
    def one(dim, shards_of):
        heights = jax.random.uniform(jax.random.fold_in(jax.random.fold_in(rng, 6), dim), (shards_of,), jnp.float32, low / len(cuts), top_value / len(cuts))
        return jnp.repeat(jnp.exp(heights), dims[dim] // shards_of).reshape((-1,) + (1,) * (len(dims) - dim - 1))

    gain = one(*cuts[0])
    for cut in cuts[1:]:
        gain = gain * one(*cut)
    return gain


def normal_values(own_key, extent, width, bound, cuts=(), dtype=jnp.bfloat16):
    values = width * jax.random.normal(own_key, extent, jnp.float32)
    if cuts:
        values = values * steps_of(own_key, extent, cuts, -0.22, 0.18)
    return jnp.clip(values, -bound, bound).astype(dtype)


def setup_inputs(seed: int = 0) -> dict:
    streams_of = jax.random.split(jax.random.key(seed), 6)
    return {
        "history": normal_values(streams_of[0], (LAGS, NR, NC), 1.0, 6.0, ((1, 16), (2, 8))),
        "rack_lag_coefficients": normal_values(streams_of[1], (LAGS, NR), 0.6, 4.0, ((1, 16),), jnp.float32),
        "class_lag_coefficients": normal_values(streams_of[2], (LAGS, NC), 0.6, 4.0, ((1, 8),), jnp.float32),
        "rack_reconcile_matrix": draw_rack_reconcile_matrix(jax.random.fold_in(streams_of[5], 71), 0),
        "class_reconcile_matrix": draw_class_reconcile_matrix(jax.random.fold_in(streams_of[5], 71), 0),
    }


def reference(history, rack_lag_coefficients, class_lag_coefficients, rack_reconcile_matrix, class_reconcile_matrix):
    predict_step = jnp.sum(history.astype(jnp.float32) * rack_lag_coefficients[:, :, None] * class_lag_coefficients[:, None, :], axis=0)
    lefthand_operand = jnp.dot(rack_reconcile_matrix, predict_step, precision=lax.Precision.HIGHEST, preferred_element_type=jnp.float32)
    return lax.dot_general(lefthand_operand, class_reconcile_matrix, (((1,), (1,)), ((), ())), precision=lax.Precision.HIGHEST, preferred_element_type=jnp.float32)
```

```python
import functools

import jax
import jax.numpy as jnp
from jax import lax
from jax.experimental import pallas as pl
from jax.experimental.pallas import tpu as pltpu
from jax.sharding import PartitionSpec as P


AXES = ("rack", "cls")


def place(index):
    rack, cls = divmod(index, 8)
    return (rack // 2 % 2 * 2 + cls // 4, cls % 4, rack // 4, rack % 2)


def index_of(x, y, z, core):
    return ((z * 2 + x // 2) * 2 + core) * 8 + x % 2 * 4 + y


def moved(step):
    return [(i, index_of(*step(*place(i)))) for i in range(128)]


Y_UP = moved(lambda x, y, z, c: (x, (y + 1) % 4, z, c))
Y_DOWN = moved(lambda x, y, z, c: (x, (y + 3) % 4, z, c))
Z_UP = moved(lambda x, y, z, c: (x, y, (z + 1) % 4, c))
Z_DOWN = moved(lambda x, y, z, c: (x, y, (z + 3) % 4, c))
X_LO = moved(lambda x, y, z, c: (x ^ 1, y, z, c))
X_HI = moved(lambda x, y, z, c: (x ^ 2, y, z, c))
CORE = moved(lambda x, y, z, c: (x, y, z, c ^ 1))

ARRIVALS = ((0, 0), (0, 1), (3, 0), (1, 0), (3, 1), (1, 1), (2, 0), (2, 1))


SMEM = pl.BlockSpec(memory_space=pltpu.SMEM)
VMEM = pl.BlockSpec(memory_space=pltpu.VMEM)


def send(array, pairs):
    return lax.ppermute(array, AXES, pairs)


def halves(a):
    top = a.astype(jnp.bfloat16)
    return top, (a - top.astype(jnp.float32)).astype(jnp.bfloat16)


def split_dot(a_hi, a_lo, b_hi, b_lo, axis):
    def dot(a, b):
        return lax.dot_general(
            a, b, (((1,), (axis,)), ((), ())), preferred_element_type=jnp.float32
        )

    return dot(a_hi, b_hi) + (dot(a_hi, b_lo) + dot(a_lo, b_hi))


def split_rows(copies):
    @pl.loop(0, 5)
    def _(i):
        for source, hi, lo, row, cols in copies:
            n = source.shape[0] // 5
            here = pl.ds(pl.multiple_of(i * n, 16), n)
            there = pl.ds(pl.multiple_of(row + i * n, 16), n)
            hi[there, cols], lo[there, cols] = halves(source[here])


def arrival_of(spot, p):
    rack, cls = spot[0], spot[1]
    dz, e = ARRIVALS[p]
    index = (rack // 4 + dz) % 4 * 2 + ((rack // 2) % 2 + e) % 2
    dy = (index % 4 + 4 - cls % 4) % 4
    other = (index // 4 + cls // 4) % 2
    return (3 * dy) % 7 + other * (1 + dy % 2)


def pair_kernel(spot, own, twin, hi, lo, pair):
    core = spot[0] % 2
    pair[core] = own[...]
    pair[1 - core] = twin[...]
    hi[...], lo[...] = halves(pair[...].reshape(-1, pair.shape[2]).T)


def turned_pair(spot, own, twin):
    rows, depth = own.shape
    return pl.pallas_call(
        pair_kernel,
        in_specs=[SMEM] + [VMEM] * 2,
        out_specs=[VMEM] * 2,
        out_shape=[jax.ShapeDtypeStruct((depth, 2 * rows), jnp.bfloat16)] * 2,
        scratch_shapes=[pltpu.VMEM((2, rows, depth), jnp.float32)],
        compiler_params=pltpu.CompilerParams(vmem_limit_bytes=16 << 20),
        cost_estimate=pl.CostEstimate(
            flops=8 * rows * depth,
            bytes_accessed=16 * rows * depth,
            transcendentals=0,
        ),
    )(spot, own, twin)


def terms_kernel(first, spot, *refs):
    pieces, (pair_hi, pair_lo), outs = refs[:8], refs[8:10], refs[10:-3]
    stack_hi, stack_lo, result = refs[-3:]
    n, rows = len(outs), pieces[0].shape[0]
    for p, piece in enumerate(pieces):
        at = arrival_of(spot, p) - first

        @pl.when(jnp.logical_and(at >= 0, at < n))
        def _(at=at, piece=piece):
            split_rows([(piece, stack_hi, stack_lo, at * rows, slice(None))])

    @pl.loop(0, n // 2)
    def _(k):
        some = pl.ds(pl.multiple_of(2 * k * rows, 16), 2 * rows)
        result[some] = split_dot(
            stack_hi[some], stack_lo[some], pair_hi[...], pair_lo[...], 0
        )

    @pl.loop(0, 5)
    def _(i):
        for o, out in enumerate(outs):
            here = pl.ds(pl.multiple_of(i * (rows // 5), 8), rows // 5)
            there = pl.ds(pl.multiple_of(o * rows + i * (rows // 5), 8), rows // 5)
            out[here] = result[there]


def block_terms(spot, pieces, pair_parts, first, n):
    rows, depth = pieces[0].shape
    half = pair_parts[0].shape[1] // 2
    return pl.pallas_call(
        functools.partial(terms_kernel, first),
        in_specs=[SMEM] + [VMEM] * 10,
        out_specs=[VMEM] * n,
        out_shape=[jax.ShapeDtypeStruct((rows, 2 * half), jnp.float32)] * n,
        scratch_shapes=[
            pltpu.VMEM((n * rows, depth), jnp.bfloat16),
            pltpu.VMEM((n * rows, depth), jnp.bfloat16),
            pltpu.VMEM((n * rows, 2 * half), jnp.float32),
        ],
        compiler_params=pltpu.CompilerParams(vmem_limit_bytes=24 << 20),
        cost_estimate=pl.CostEstimate(
            flops=12 * n * rows * half * depth,
            bytes_accessed=8 * n * rows * depth,
            transcendentals=0,
        ),
    )(spot, *pieces, *pair_parts)


def split_kernel(places, *refs):
    pieces, (hi, lo) = refs[:-2], refs[-2:]
    split_rows(
        [
            (piece, hi, lo, row, pl.ds(col, piece.shape[1]))
            for (row, col), piece in zip(places, pieces)
        ]
    )


def split_panel(own, twin):
    places, pieces = [], []
    for side, blocks in enumerate((own, twin)):
        for k, block in enumerate(blocks):
            rows = sum(part.shape[0] for part in block)
            row = side * rows
            for part in block:
                depth = part.shape[1]
                places.append((row, k * depth))
                pieces.append(part)
                row += part.shape[0]
    shape = (2 * rows, len(own) * depth)
    return pl.pallas_call(
        functools.partial(split_kernel, tuple(places)),
        in_specs=[VMEM] * len(pieces),
        out_specs=[VMEM] * 2,
        out_shape=[jax.ShapeDtypeStruct(shape, jnp.bfloat16)] * 2,
        compiler_params=pltpu.CompilerParams(vmem_limit_bytes=24 << 20),
        cost_estimate=pl.CostEstimate(
            flops=4 * shape[0] * shape[1],
            bytes_accessed=8 * shape[0] * shape[1],
            transcendentals=0,
        ),
    )(*pieces)


def product_kernel(begun, spot, *refs):
    parts, panels, sums = refs[:8], refs[8 : -5 - 2 * begun], refs[-5 - 2 * begun : -5]
    mine, theirs, b_hi, b_lo, result = refs[-5:]
    rows, depth = mine.shape[0], parts[0].shape[1]
    copies = []
    for p, part in enumerate(parts):
        at = pl.ds(pl.multiple_of(arrival_of(spot, p) * depth, 128), depth)
        copies.append((part, b_hi, b_lo, 0, at))
    split_rows(copies)

    size = result.shape[1]

    @pl.loop(0, result.shape[0])
    def _(i):
        some = pl.ds(pl.multiple_of(i * size, 8), size)
        total, start = None, 8 * depth - sum(a.shape[1] for a in panels[0::2])
        start = start if begun else 0
        for a_hi, a_lo in zip(panels[0::2], panels[1::2]):
            at = pl.ds(start, a_hi.shape[1])
            start += a_hi.shape[1]
            term = split_dot(a_hi[some], a_lo[some], b_hi[:, at], b_lo[:, at], 1)
            total = term if total is None else total + term
        result[i] = total

    for i, out in enumerate((mine, theirs)):
        for j in range(rows // size):
            at = pl.ds(j * size, size)
            part = result[i * (rows // size) + j]
            out[at] = part + sums[i][at] if begun else part


def product(spot, parts, panels, sums=()):
    size, depth = parts[0].shape
    rows = panels[0].shape[0] // 2
    wide = sum(a.shape[1] for a in panels[0::2])
    return pl.pallas_call(
        functools.partial(product_kernel, bool(sums)),
        in_specs=[SMEM] + [VMEM] * (8 + len(panels) + len(sums)),
        out_specs=[VMEM] * 2,
        out_shape=[jax.ShapeDtypeStruct((rows, size), jnp.float32)] * 2,
        scratch_shapes=[
            pltpu.VMEM((size, 8 * depth), jnp.bfloat16),
            pltpu.VMEM((size, 8 * depth), jnp.bfloat16),
            pltpu.VMEM((4, rows // 2, size), jnp.float32),
        ],
        compiler_params=pltpu.CompilerParams(vmem_limit_bytes=24 << 20),
        cost_estimate=pl.CostEstimate(
            flops=12 * rows * size * wide,
            bytes_accessed=4 * (2 * rows + size) * wide,
            transcendentals=0,
        ),
    )(spot, *parts, *panels, *sums)


def step(history, rack_coef, class_coef, rack_matrix, class_matrix):
    rack, cls = lax.axis_index("rack"), lax.axis_index("cls")
    spot = jnp.stack([rack, cls]).astype(jnp.int32)
    size = rack_matrix.shape[0] // 2
    forecast = jnp.sum(
        history.astype(jnp.float32) * rack_coef[:, :, None] * class_coef[:, None, :],
        axis=0,
    )
    c0, c1, r = class_matrix[:size], class_matrix[size:], rack_matrix
    pair = turned_pair(spot, forecast, send(forecast, CORE))

    def gather(own, up, down, across):
        other = send(own, across)
        below, above = send(own, up), send(own, down)
        other_below = send(other, up)
        other_above = send(other, down)
        far = send(below, up)
        other_far = send(other_above, down)
        return own, other, below, above, other_below, other_above, far, other_far

    def scatter(t):
        up, down = send(t[6], Y_UP), send(t[7], Y_DOWN)
        e = send(t[5], Y_UP)
        f = send(t[4] + down, Y_DOWN)
        g = send(t[3] + up, Y_UP)
        i = send(t[2], Y_DOWN)
        return t[0] + g + i + send(t[1] + e + f, X_LO)

    def gather_other(own):
        other = send(own, X_LO)
        below, above = send(other, Y_UP), send(other, Y_DOWN)
        return {"": other, "b": below, "a": above, "f": send(above, Y_DOWN)}

    below, above = send(r, Y_UP), send(r, Y_DOWN)
    far = send(below, Y_UP)
    sides = [gather_other(r[h * size : (h + 1) * size]) for h in (0, 1)]
    panel = [(r,), None, (below,), (above,), None, None, (far,), None]
    twin = [
        (send(r, CORE),),
        None,
        (send(below, CORE),),
        (send(above, CORE),),
        None,
        None,
        (send(far, CORE),),
        None,
    ]
    for k, kind in ((1, ""), (4, "b"), (5, "a"), (7, "f")):
        panel[k] = tuple(side[kind] for side in sides)
        twin[k] = tuple(send(side[kind], CORE) for side in sides)
    gathered = []
    for c in (c0, c1):
        pieces = gather(c, Z_UP, Z_DOWN, X_HI)
        near = block_terms(spot, pieces, pair, 4, 4)
        rest = block_terms(spot, pieces, pair, 0, 4)
        h = scatter((*rest, *near))
        gathered.append(gather(h, Z_UP, Z_DOWN, X_HI))
    panel0 = split_panel(panel[:6], twin[:6])
    panel1 = split_panel(panel[6:], twin[6:])
    first = product(spot, gathered[0], panel0)
    first = product(spot, gathered[0], panel1, first)
    second = product(spot, gathered[1], (*panel0, *panel1))
    mine, theirs = zip(first, second)
    other = [send(a, CORE) for a in theirs]
    return jnp.where(
        rack % 2 == 0,
        jnp.concatenate([*mine, *other], axis=1),
        jnp.concatenate([*other, *mine], axis=1),
    )


def solution(mesh):
    placed = (
        P(None, "rack", "cls"),
        P(None, "rack"),
        P(None, "cls"),
        P("rack", "cls"),
        P("rack", "cls"),
    )
    return jax.shard_map(
        step, mesh=mesh, in_specs=placed, out_specs=P("rack", "cls"), check_vma=False
    )
```
